128 devices in a mesh: dp: 16 (over y, x), expert: 8 (over z, core).
Axes of the slice: x: 4, y: 4, z: 4, core: 2. Of those that a mesh axis runs over, the one named last changes fastest.
Arguments:
- tokens: bfloat16 [4096, 4096], P('dp', 'expert'), may hold values from -100 to 100
- w_gate: bfloat16 [8, 4096, 14336], P('expert', None, 'dp'), may hold values from -0.09375 to 0.09375
- w_up: bfloat16 [8, 4096, 14336], P('expert', None, 'dp'), may hold values from -0.09375 to 0.09375
- w_down: bfloat16 [8, 14336, 4096], P('expert', 'dp'), may hold values from -0.046875 to 0.046875
- pick_block: int32 [8, 8], replicated, may hold values from 0 to 3
- pick_live: int32 [8, 8], replicated, may hold values from 0 to 1, as said below
- combine_weight: float32 [8, 8], replicated, may hold values from 0.25 to 1
Outputs:
- combined: bfloat16 [4096, 4096], P('dp', 'expert')
The draws below stay inside these ranges and needn't reach their ends.
Inputs may be any that keep to these rules, and one draw needn't show every extreme that they name: `pick_live`: each expert takes at least one block, and some expert takes a block from every pair of dp rows.
All inputs are finite; a program needn't handle non-finite values.
Results may differ from the reference program's by a relative error of at most 0.02.
Values may be sent and summed in bfloat16 or wider, within the bound.
A program may use at most 128 MiB of HBM per device.

```python
import math
import jax
import jax.numpy as jnp
from jax import lax

D = 4096
FF = 14336
BLOCK = 128
BLK_ROW = 2
EXPERTS = 8
PAIRS = 8
HID_DEV = 896
TOKENS = 4096
N_DP = 16


def draw_tokens(key, part):
    key_base, key_row, key_col = jax.random.split(key, 3)
    col_scale = jnp.exp(jax.random.uniform(key_col, (1, D), jnp.float32, math.log(0.5), math.log(2.0)))
    base_values = jax.random.normal(key_base, (TOKENS, D), jnp.float32)
    row_scale = jnp.exp(jax.random.uniform(key_row, (TOKENS, 1), jnp.float32, math.log(0.3), math.log(3.0)))
    values = jnp.clip(base_values * row_scale * col_scale, -100.0, 100.0)
    return values.astype(jnp.bfloat16)


def draw_pick_live(key, part):
    key_count, key_full, key_order = jax.random.split(key, 3)
    counts = jax.random.randint(key_count, (EXPERTS,), 1, PAIRS + 1)
    full_one = jax.random.randint(key_full, (), 0, EXPERTS)
    counts = jnp.where(jnp.arange(EXPERTS) == full_one, PAIRS, counts)
    ranking = jax.vmap(lambda sub_key: jax.random.permutation(sub_key, PAIRS))(jax.random.split(key_order, EXPERTS))
    return (ranking < counts[:, None]).astype(jnp.int32)


def set_ends(array, own_key, smallest, top_value):
    index_at = [jax.random.randint(jax.random.fold_in(own_key, axis), (), 0, length) for axis, length in enumerate(array.shape)]
    longest = array.shape.index(max(array.shape))
    beside = index_at[:longest] + [(index_at[longest] + 1) % array.shape[longest]] + index_at[longest + 1:]
    return array.at[tuple(index_at)].set(smallest).at[tuple(beside)].set(top_value)


def level_of(stream_key, dims, shards, smallest, high):
    def one(position, shards_of):
        steps = jax.random.uniform(jax.random.fold_in(jax.random.fold_in(stream_key, 6), position), (shards_of,), jnp.float32, smallest / len(shards), high / len(shards))
        return jnp.repeat(jnp.exp(steps), dims[position] // shards_of).reshape((-1,) + (1,) * (len(dims) - position - 1))

    level = one(*shards[0])
    for cut in shards[1:]:
        level = level * one(*cut)
    return level


def scatter_about(rng, shape, scale, most, cuts=(), kind=jnp.bfloat16):
    entries = jax.random.normal(rng, shape, jnp.float32) * scale
    if len(cuts) > 0:
        entries = level_of(rng, shape, cuts, -0.22, 0.18) * entries
    return jnp.clip(entries, min=-most, max=most).astype(kind)


def setup_inputs(seed: int = 0) -> dict:
    seeds = jax.random.split(jax.random.key(seed), 8)
    return {
        "tokens": draw_tokens(jax.random.fold_in(seeds[7], 71), 0),
        "w_gate": scatter_about(seeds[1], (EXPERTS, D, FF), D ** -0.5, 0.09375, ((0, 8), (2, 16))),
        "w_up": scatter_about(seeds[2], (EXPERTS, D, FF), D ** -0.5, 0.09375, ((0, 8), (2, 16))),
        "w_down": scatter_about(seeds[3], (EXPERTS, FF, D), FF ** -0.5, 0.046875, ((0, 8), (1, 16))),
        "pick_block": set_ends(jax.random.randint(seeds[4], (EXPERTS, PAIRS), 0, 2 * BLK_ROW), jax.random.fold_in(seeds[4], 1), 0, (2 * BLK_ROW) - 1).astype(jnp.int32),
        "pick_live": draw_pick_live(jax.random.fold_in(seeds[7], 71), 0),
        "combine_weight": jnp.clip(jnp.exp(jax.random.uniform(seeds[6], (EXPERTS, PAIRS), jnp.float32, math.log(0.25), math.log(1.0))), 0.25, 1.0),
    }


def reference(tokens, w_gate, w_up, w_down, pick_block, pick_live, combine_weight):
    tokens_f32 = tokens.astype(jnp.float32)
    inv_rms = lax.rsqrt(lax.optimization_barrier(jnp.mean(tokens_f32 * tokens_f32, axis=1, keepdims=True)) + 1e-05)
    normed = (tokens_f32 * inv_rms).astype(jnp.bfloat16)
    blocks = normed.reshape(TOKENS // BLOCK, BLOCK, D)
    combined = jnp.zeros((TOKENS // BLOCK, BLOCK, D), jnp.float32)
    pair_ids = jnp.arange(PAIRS, dtype=jnp.int32)
    for expert in range(EXPERTS):
        block_index = (2 * BLK_ROW * pair_ids + pick_block[expert]).astype(jnp.int32)
        live_mask = pick_live[expert] == 1
        chosen = jnp.where(live_mask[:, None, None], blocks[block_index], jnp.zeros((), jnp.bfloat16))
        chosen = chosen.reshape(PAIRS * BLOCK, D)
        gate_proj = jnp.dot(chosen, w_gate[expert], preferred_element_type=jnp.float32)
        up_proj = jnp.dot(chosen, w_up[expert], preferred_element_type=jnp.float32)
        hidden = (jax.nn.silu(gate_proj) * up_proj).astype(jnp.bfloat16)
        summed = jnp.zeros((PAIRS * BLOCK, D), jnp.float32)
        for group_index in range(N_DP):
            lower = group_index * HID_DEV
            partial_value = jnp.dot(hidden[:, lower:lower + HID_DEV], w_down[expert, lower:lower + HID_DEV], preferred_element_type=jnp.float32).astype(jnp.bfloat16)
            summed = summed + lax.optimization_barrier(partial_value).astype(jnp.float32)
        expert_out = lax.optimization_barrier(summed.astype(jnp.bfloat16)).astype(jnp.float32)
        weighting = jnp.where(live_mask, combine_weight[expert], jnp.zeros((), jnp.float32))
        combined = combined.at[block_index].add(weighting[:, None, None] * expert_out.reshape(PAIRS, BLOCK, D))
    return combined.astype(jnp.bfloat16).reshape(TOKENS, D)
```

```python
import functools

import jax
import jax.numpy as jnp
from jax import lax
from jax.experimental import pallas as pl
from jax.experimental.pallas import tpu as pltpu
from jax.sharding import PartitionSpec as P

BLOCK = 128
HALF = BLOCK // 2
SUB = 16
RING = 4
BF16 = jnp.bfloat16
F32 = jnp.float32


def layer_kernel(
    expert_count,
    tok,
    w_gate,
    w_up,
    w_down,
    pick,
    live,
    weight,
    out,
    pair_buf,
    send_buf,
    arrived,
    rows,
    w_gu,
    w_dn,
    hidden,
    part,
    from_minus,
    from_plus,
    far_minus,
    far_plus,
    mid,
    mid_minus,
    mid_plus,
    mid_far_minus,
    mid_far_plus,
    finished,
    returned,
    merged,
    send_sem,
    recv_sem,
    weight_sem,
    local_sem,
):
    position = lax.axis_index("dp")
    expert = lax.axis_index("expert")
    x = lax.rem(position, RING)
    y = position // RING
    half = lax.rem(position, 2)
    pair = position // 2
    partner = position + 1 - 2 * half
    x_plus = y * RING + lax.rem(x + 1, RING)
    x_minus = y * RING + lax.rem(x + RING - 1, RING)
    y_plus = lax.rem(y + 1, RING) * RING + x
    y_minus = lax.rem(y + RING - 1, RING) * RING + x
    near = ((x_plus, x_minus), (y_plus, y_minus))
    wide = ((y_plus, y_minus), (x_plus, x_minus))
    lanes = tok.shape[-1]
    width = lanes * expert_count
    hid_tiles = w_gate.shape[1] // 128
    peers = (4, 3, 5, 2, 6, 1, 7)

    weight_copies = []
    for tile in range(hid_tiles):
        for which, source in enumerate((w_gate, w_up)):
            weight_copies.append(
                pltpu.make_async_copy(
                    source.at[:, pl.ds(tile * 128, 128)],
                    w_gu.at[tile, :, pl.ds(which * 128, 128)],
                    weight_sem.at[2 * tile + which],
                )
            )
    weight_copies.append(pltpu.make_async_copy(w_down, w_dn, weight_sem.at[2 * hid_tiles]))

    barrier = pltpu.get_barrier_semaphore()
    for target in (x_plus, x_minus, y_plus, y_minus):
        pl.semaphore_signal(
            barrier, inc=1, device_id={"dp": target}, device_id_type=pl.DeviceIdType.MESH
        )
    for offset in peers:
        pl.semaphore_signal(
            barrier,
            inc=1,
            device_id={"expert": lax.rem(expert + offset, expert_count)},
            device_id_type=pl.DeviceIdType.MESH,
        )
    pl.semaphore_wait(barrier, 4 + len(peers))

    copies = {}

    def send(key, source, target, device):
        number = len(copies)
        copy = pltpu.make_async_remote_copy(
            src_ref=source,
            dst_ref=target,
            send_sem=send_sem.at[number],
            recv_sem=recv_sem.at[number],
            device_id=device,
            device_id_type=pl.DeviceIdType.MESH,
        )
        copy.start()
        copies[key] = copy

    def arrive(*key):
        copies[key].wait_recv()

    send(("pair",), tok.at[:, 1 - half], pair_buf.at[pl.ds(2 * half, 2)], {"dp": partner})
    own_copy = pltpu.make_async_copy(
        tok.at[:, half], pair_buf.at[pl.ds(2 * half, 2)], local_sem.at[0]
    )
    own_copy.start()
    for copy in weight_copies:
        copy.start()
    own_copy.wait()
    arrive("pair")

    def choose(target):
        chosen = pair_buf[pick[target, pair]].astype(F32)
        return (chosen * live[target, pair].astype(F32)).astype(BF16)

    for offset in peers:
        target = lax.rem(expert + offset, expert_count)
        send_buf[offset] = choose(target)
        send(("out", offset), send_buf.at[offset], arrived.at[expert], {"expert": target})
    arrived[expert] = choose(expert)
    for offset in peers:
        arrive("out", offset)

    for piece in range(HALF // SUB):
        square_sum = jnp.zeros((SUB, 1), F32)
        for source in range(expert_count):
            values = arrived[source, pl.ds(piece * SUB, SUB)].astype(F32)
            square_sum += jnp.sum(values * values, axis=1, keepdims=True)
        inv_rms = lax.rsqrt(square_sum / width + 1e-05)
        for source in range(expert_count):
            values = arrived[source, pl.ds(piece * SUB, SUB)].astype(F32)
            rows[0, piece // 2, 0, piece % 2, :, pl.ds(source * lanes, lanes)] = (
                values * inv_rms
            ).astype(BF16)

    def spread_wide(c, r):
        send(("rows", 2, c, r), rows.at[0, c, r], rows.at[2, c, r], {"dp": wide[c][0]})
        send(("rows", 1, c, r), rows.at[0, c, r], rows.at[1, c, r], {"dp": wide[c][1]})

    def forward_wide(c, r):
        arrive("rows", 2, c, r)
        send(("far", c, r, 0), rows.at[2, c, r, 0], rows.at[3, c, r, 0], {"dp": wide[c][0]})
        arrive("rows", 1, c, r)
        send(("far", c, r, 1), rows.at[1, c, r, 1], rows.at[3, c, r, 1], {"dp": wide[c][1]})

    def experts(s):
        def gate_up(tile, carry):
            group = rows[s].reshape(2 * RING * 2 * SUB, width)
            both = jnp.dot(group, w_gu[tile], preferred_element_type=F32)
            gate = both[:, :128]
            value = gate * (1.0 / (1.0 + jnp.exp(-gate))) * both[:, 128:]
            hidden[:, pl.ds(pl.multiple_of(tile * 128, 128), 128)] = value.astype(BF16)
            return carry

        lax.fori_loop(0, hid_tiles, gate_up, 0)

        def down(tile, carry):
            columns = pl.ds(pl.multiple_of(tile * 512, 512), 512)
            value = jnp.dot(hidden[...], w_dn[:, columns], preferred_element_type=F32)
            part[s, :, :, :, :, columns] = value.astype(BF16).reshape(2, RING, 2, SUB, 512)
            return carry

        lax.fori_loop(0, width // 512, down, 0)

    for c in range(2):
        send(("near", c, 2), rows.at[0, c, 0], rows.at[0, c, 2], {"dp": near[c][0]})
        send(("near", c, 1), rows.at[0, c, 0], rows.at[0, c, 1], {"dp": near[c][1]})
    for c in range(2):
        spread_wide(c, 0)
    for c in range(2):
        arrive("near", c, 2)
        send(("nearfar", c, 0), rows.at[0, c, 2, 0], rows.at[0, c, 3, 0], {"dp": near[c][0]})
        arrive("near", c, 1)
        send(("nearfar", c, 1), rows.at[0, c, 1, 1], rows.at[0, c, 3, 1], {"dp": near[c][1]})
    for r in (1, 2):
        for c in range(2):
            spread_wide(c, r)
    for c in range(2):
        arrive("nearfar", c, 0)
        arrive("nearfar", c, 1)
        spread_wide(c, 3)
    for c in range(2):
        forward_wide(c, 0)
    for copy in weight_copies:
        copy.wait()
    experts(0)
    for r in (1, 2, 3):
        for c in range(2):
            forward_wide(c, r)
    experts(1)
    for c in range(2):
        send(("half", c, 1), part.at[1, c, :, 1], from_minus.at[c, :, 1], {"dp": wide[c][0]})
    experts(2)
    for c in range(2):
        send(("half", c, 0), part.at[2, c, :, 0], from_plus.at[c, :, 0], {"dp": wide[c][1]})
    for r in range(RING):
        for c in range(2):
            arrive("far", c, r, 0)
            arrive("far", c, r, 1)
    experts(3)
    order = (3, 1, 2, 0)
    for r in order:
        for c in range(2):
            send(("sumfar", c, r, 0), part.at[3, c, r, 0], far_minus.at[c, r], {"dp": wide[c][0]})
            send(("sumfar", c, r, 1), part.at[3, c, r, 1], far_plus.at[c, r], {"dp": wide[c][1]})
    for r in order:
        for c in range(2):
            arrive("sumfar", c, r, 0)
            part[1, c, r, 0] = (part[1, c, r, 0].astype(F32) + far_minus[c, r].astype(F32)).astype(
                BF16
            )
            send(
                ("sum", c, r, 0), part.at[1, c, r, 0], from_minus.at[c, r, 0], {"dp": wide[c][0]}
            )
            arrive("sumfar", c, r, 1)
            part[2, c, r, 1] = (part[2, c, r, 1].astype(F32) + far_plus[c, r].astype(F32)).astype(
                BF16
            )
            send(("sum", c, r, 1), part.at[2, c, r, 1], from_plus.at[c, r, 1], {"dp": wide[c][1]})
    for c in range(2):
        arrive("half", c, 1)
        arrive("half", c, 0)

    def row_sum(c, r, piece):
        return (
            part[0, c, r, piece].astype(F32)
            + from_minus[c, r, piece].astype(F32)
            + from_plus[c, r, piece].astype(F32)
        )

    for c in range(2):
        arrive("sum", c, 3, 0)
        arrive("sum", c, 3, 1)
        for piece in range(2):
            mid[c, 3, piece] = row_sum(c, 3, piece).astype(BF16)
            target = (mid_far_minus, mid_far_plus)[piece]
            send(("midfar", c, piece), mid.at[c, 3, piece], target.at[c], {"dp": near[c][piece]})
    for c in range(2):
        arrive("sum", c, 1, 0)
        arrive("sum", c, 1, 1)
        mid[c, 1, 1] = row_sum(c, 1, 1).astype(BF16)
        send(("mid", c, 1), mid.at[c, 1, 1], mid_minus.at[c, 1], {"dp": near[c][0]})
        arrive("sum", c, 2, 0)
        arrive("sum", c, 2, 1)
        mid[c, 2, 0] = row_sum(c, 2, 0).astype(BF16)
        send(("mid", c, 0), mid.at[c, 2, 0], mid_plus.at[c, 0], {"dp": near[c][1]})
    for c in range(2):
        arrive("midfar", c, 0)
        mid[c, 1, 0] = (row_sum(c, 1, 0) + mid_far_minus[c].astype(F32)).astype(BF16)
        send(("midsum", c, 0), mid.at[c, 1, 0], mid_minus.at[c, 0], {"dp": near[c][0]})
        arrive("midfar", c, 1)
        mid[c, 2, 1] = (row_sum(c, 2, 1) + mid_far_plus[c].astype(F32)).astype(BF16)
        send(("midsum", c, 1), mid.at[c, 2, 1], mid_plus.at[c, 1], {"dp": near[c][1]})
    for c in range(2):
        arrive("sum", c, 0, 0)
        arrive("sum", c, 0, 1)
        arrive("mid", c, 0)
        arrive("mid", c, 1)
        arrive("midsum", c, 0)
        arrive("midsum", c, 1)
        for piece in range(2):
            total = (
                row_sum(c, 0, piece)
                + mid_minus[c, piece].astype(F32)
                + mid_plus[c, piece].astype(F32)
            ).astype(BF16)
            first_row = (2 * c + piece) * SUB
            for target in range(expert_count):
                finished[target, pl.ds(first_row, SUB)] = total[
                    :, target * lanes : (target + 1) * lanes
                ]

    for offset in peers:
        target = lax.rem(expert + offset, expert_count)
        send(("back", offset), finished.at[target], returned.at[expert], {"expert": target})
    returned[expert] = finished[expert]
    for offset in peers:
        arrive("back", offset)

    for piece in range(HALF // SUB):
        window = pl.ds(piece * SUB, SUB)
        totals = [jnp.zeros((SUB, lanes), F32) for _ in range(4)]
        for source in range(expert_count):
            values = returned[source, window].astype(F32)
            block = pick[source, pair]
            scale = jnp.where(live[source, pair] == 1, weight[source, pair], 0.0)
            for slot in range(4):
                totals[slot] = totals[slot] + jnp.where(block == slot, scale, 0.0) * values
        for slot in range(4):
            merged[slot, window] = totals[slot].astype(BF16)
    send(
        ("final",), merged.at[pl.ds(2 * (1 - half), 2)], out.at[:, half], {"dp": partner}
    )
    last_copy = pltpu.make_async_copy(
        merged.at[pl.ds(2 * half, 2)], out.at[:, half], local_sem.at[1]
    )
    last_copy.start()
    for key, copy in copies.items():
        copy.wait_send()
    last_copy.wait()
    arrive("final")


def on_device(tokens, w_gate, w_up, w_down, pick_block, pick_live, combine_weight):
    expert_count = lax.axis_size("expert")
    lanes = tokens.shape[1]
    width = lanes * expert_count
    group = w_gate.shape[2]
    hid_tiles = group // 128
    hbm = pl.BlockSpec(memory_space=pl.ANY)
    smem = pl.BlockSpec(memory_space=pltpu.SMEM)
    copy_count = 128
    result = pl.pallas_call(
        functools.partial(layer_kernel, expert_count),
        out_shape=jax.ShapeDtypeStruct((2, 2, HALF, lanes), BF16),
        in_specs=[hbm, hbm, hbm, hbm, smem, smem, smem],
        out_specs=hbm,
        scratch_shapes=[
            pltpu.VMEM((4, HALF, lanes), BF16),
            pltpu.VMEM((expert_count, HALF, lanes), BF16),
            pltpu.VMEM((expert_count, HALF, lanes), BF16),
            pltpu.VMEM((RING, 2, RING, 2, SUB, width), BF16),
            pltpu.VMEM((hid_tiles, width, 256), BF16),
            pltpu.VMEM((group, width), BF16),
            pltpu.VMEM((2 * RING * 2 * SUB, group), BF16),
            pltpu.VMEM((RING, 2, RING, 2, SUB, width), BF16),
            pltpu.VMEM((2, RING, 2, SUB, width), BF16),
            pltpu.VMEM((2, RING, 2, SUB, width), BF16),
            pltpu.VMEM((2, RING, SUB, width), BF16),
            pltpu.VMEM((2, RING, SUB, width), BF16),
            pltpu.VMEM((2, RING, 2, SUB, width), BF16),
            pltpu.VMEM((2, 2, SUB, width), BF16),
            pltpu.VMEM((2, 2, SUB, width), BF16),
            pltpu.VMEM((2, SUB, width), BF16),
            pltpu.VMEM((2, SUB, width), BF16),
            pltpu.VMEM((expert_count, HALF, lanes), BF16),
            pltpu.VMEM((expert_count, HALF, lanes), BF16),
            pltpu.VMEM((4, HALF, lanes), BF16),
            pltpu.SemaphoreType.DMA((copy_count,)),
            pltpu.SemaphoreType.DMA((copy_count,)),
            pltpu.SemaphoreType.DMA((2 * hid_tiles + 1,)),
            pltpu.SemaphoreType.DMA((2,)),
        ],
        compiler_params=pltpu.CompilerParams(
            collective_id=0, has_side_effects=True, vmem_limit_bytes=60 * 1024 * 1024
        ),
        name="moe_layer",
    )(
        tokens.reshape(2, 2, HALF, lanes),
        w_gate[0],
        w_up[0],
        w_down[0],
        pick_block,
        pick_live,
        combine_weight,
    )
    return result.reshape(tokens.shape)


def solution(mesh):
    in_specs = (
        P("dp", "expert"),
        P("expert", None, "dp"),
        P("expert", None, "dp"),
        P("expert", "dp", None),
        P(),
        P(),
        P(),
    )
    return jax.shard_map(
        on_device, mesh=mesh, in_specs=in_specs, out_specs=P("dp", "expert"), check_vma=False
    )
```

```python
import functools

import jax
import jax.numpy as jnp
from jax import lax
from jax.experimental import pallas as pl
from jax.experimental.pallas import tpu as pltpu
from jax.sharding import PartitionSpec as P

BLOCK = 128
HALF = BLOCK // 2
SUB = 16
RING = 4
DOWN = 512
BF16 = jnp.bfloat16
F32 = jnp.float32


def layer_kernel(
    expert_count,
    tok,
    w_gate,
    w_up,
    w_down,
    pick,
    live,
    weight,
    out,
    pair_first,
    pair_second,
    send_buf,
    arrived,
    rows,
    w_gu,
    w_dn,
    hidden,
    part,
    from_minus,
    from_plus,
    far_minus,
    far_plus,
    mid,
    mid_minus,
    mid_plus,
    mid_far_minus,
    mid_far_plus,
    finished,
    returned,
    merged,
    send_sem,
    recv_sem,
    weight_sem,
    local_sem,
):
    position = lax.axis_index("dp")
    expert = lax.axis_index("expert")
    x = lax.rem(position, RING)
    y = position // RING
    half = lax.rem(position, 2)
    pair = position // 2
    partner = position + 1 - 2 * half
    x_plus = y * RING + lax.rem(x + 1, RING)
    x_minus = y * RING + lax.rem(x + RING - 1, RING)
    y_plus = lax.rem(y + 1, RING) * RING + x
    y_minus = lax.rem(y + RING - 1, RING) * RING + x
    near = ((x_plus, x_minus), (y_plus, y_minus))
    wide = ((y_plus, y_minus), (x_plus, x_minus))
    lanes = tok.shape[-1]
    width = lanes * expert_count
    hid_tiles = w_gate.shape[1] // 128
    peers = (4, 3, 5, 2, 6, 1, 7)

    weight_copies = []
    for tile in range(hid_tiles):
        for which, source in enumerate((w_gate, w_up)):
            weight_copies.append(
                pltpu.make_async_copy(
                    source.at[:, pl.ds(tile * 128, 128)],
                    w_gu.at[tile, :, pl.ds(which * 128, 128)],
                    weight_sem.at[2 * tile + which],
                )
            )
    weight_copies.append(pltpu.make_async_copy(w_down, w_dn, weight_sem.at[2 * hid_tiles]))

    pair_bufs = (pair_first, pair_second)
    barrier = pltpu.get_barrier_semaphore()
    for target in (x_plus, x_minus, y_plus, y_minus):
        pl.semaphore_signal(
            barrier, inc=1, device_id={"dp": target}, device_id_type=pl.DeviceIdType.MESH
        )
    for offset in peers:
        pl.semaphore_signal(
            barrier,
            inc=1,
            device_id={"expert": lax.rem(expert + offset, expert_count)},
            device_id_type=pl.DeviceIdType.MESH,
        )
    pl.semaphore_wait(barrier, 4 + len(peers))

    copies = {}

    def send(key, source, target, device):
        number = len(copies)
        copy = pltpu.make_async_remote_copy(
            src_ref=source,
            dst_ref=target,
            send_sem=send_sem.at[number],
            recv_sem=recv_sem.at[number],
            device_id=device,
            device_id_type=pl.DeviceIdType.MESH,
        )
        copy.start()
        copies[key] = copy

    def arrive(*key):
        copies[key].wait_recv()

    for c in range(2):
        send(
            ("pair", c),
            tok.at[:, 1 - half, c],
            pair_bufs[c].at[pl.ds(2 * half, 2)],
            {"dp": partner},
        )
    own_copies = [
        pltpu.make_async_copy(
            tok.at[:, half, c], pair_bufs[c].at[pl.ds(2 * half, 2)], local_sem.at[c]
        )
        for c in range(2)
    ]
    for copy in own_copies:
        copy.start()

    def choose(target, c):
        chosen = pair_bufs[c][pick[target, pair]].astype(F32)
        return (chosen * live[target, pair].astype(F32)).astype(BF16)

    for c in range(2):
        own_copies[c].wait()
        arrive("pair", c)
        for offset in peers:
            target = lax.rem(expert + offset, expert_count)
            send_buf[c, offset] = choose(target, c)
            send(
                ("out", c, offset),
                send_buf.at[c, offset],
                arrived.at[c, expert],
                {"expert": target},
            )
        arrived[c, expert] = choose(expert, c)
    for copy in weight_copies:
        copy.start()

    def normalise(c):
        for piece in range(2):
            window = pl.ds(piece * SUB, SUB)
            square_sum = jnp.zeros((SUB, 1), F32)
            for source in range(expert_count):
                values = arrived[c, source, window].astype(F32)
                square_sum += jnp.sum(values * values, axis=1, keepdims=True)
            inv_rms = lax.rsqrt(square_sum / width + 1e-05)
            for source in range(expert_count):
                values = arrived[c, source, window].astype(F32)
                rows[0, c, 0, piece, :, pl.ds(source * lanes, lanes)] = (values * inv_rms).astype(
                    BF16
                )

    def spread_wide(c, r):
        send(("rows", 2, c, r), rows.at[0, c, r], rows.at[2, c, r], {"dp": wide[c][0]})
        send(("rows", 1, c, r), rows.at[0, c, r], rows.at[1, c, r], {"dp": wide[c][1]})

    def forward_wide(c, r):
        arrive("rows", 2, c, r)
        send(("far", c, r, 0), rows.at[2, c, r, 0], rows.at[3, c, r, 0], {"dp": wide[c][0]})
        arrive("rows", 1, c, r)
        send(("far", c, r, 1), rows.at[1, c, r, 1], rows.at[3, c, r, 1], {"dp": wide[c][1]})

    def experts(s):
        group = rows[s].reshape(2 * RING * 2 * SUB, width)
        for tile in range(hid_tiles):
            both = jnp.dot(group, w_gu[tile], preferred_element_type=F32)
            gate = both[:, :128]
            value = gate * (1.0 / (1.0 + jnp.exp(-gate))) * both[:, 128:]
            hidden[:, tile * 128 : (tile + 1) * 128] = value.astype(BF16)
        for tile in range(width // DOWN):
            columns = pl.ds(tile * DOWN, DOWN)
            value = jnp.dot(hidden[...], w_dn[:, columns], preferred_element_type=F32)
            part[s, :, :, :, :, columns] = value.astype(BF16).reshape(2, RING, 2, SUB, DOWN)

    for c in range(2):
        for offset in peers:
            arrive("out", c, offset)
        normalise(c)
        send(("near", c, 2), rows.at[0, c, 0], rows.at[0, c, 2], {"dp": near[c][0]})
        send(("near", c, 1), rows.at[0, c, 0], rows.at[0, c, 1], {"dp": near[c][1]})
        spread_wide(c, 0)
    for c in range(2):
        arrive("near", c, 2)
        send(("nearfar", c, 0), rows.at[0, c, 2, 0], rows.at[0, c, 3, 0], {"dp": near[c][0]})
        arrive("near", c, 1)
        send(("nearfar", c, 1), rows.at[0, c, 1, 1], rows.at[0, c, 3, 1], {"dp": near[c][1]})
    for r in (1, 2):
        for c in range(2):
            spread_wide(c, r)
    for c in range(2):
        arrive("nearfar", c, 0)
        arrive("nearfar", c, 1)
        spread_wide(c, 3)
    for c in range(2):
        forward_wide(c, 0)
    for copy in weight_copies:
        copy.wait()
    experts(0)
    for r in (1, 2, 3):
        for c in range(2):
            forward_wide(c, r)
    experts(1)
    for c in range(2):
        send(("half", c, 1), part.at[1, c, :, 1], from_minus.at[c, :, 1], {"dp": wide[c][0]})
    experts(2)
    for c in range(2):
        send(("half", c, 0), part.at[2, c, :, 0], from_plus.at[c, :, 0], {"dp": wide[c][1]})
    for r in range(RING):
        for c in range(2):
            arrive("far", c, r, 0)
            arrive("far", c, r, 1)
    experts(3)
    order = (3, 1, 2, 0)
    for r in order:
        for c in range(2):
            send(("sumfar", c, r, 0), part.at[3, c, r, 0], far_minus.at[c, r], {"dp": wide[c][0]})
            send(("sumfar", c, r, 1), part.at[3, c, r, 1], far_plus.at[c, r], {"dp": wide[c][1]})
    for r in order:
        for c in range(2):
            arrive("sumfar", c, r, 0)
            part[1, c, r, 0] = (part[1, c, r, 0].astype(F32) + far_minus[c, r].astype(F32)).astype(
                BF16
            )
            send(
                ("sum", c, r, 0), part.at[1, c, r, 0], from_minus.at[c, r, 0], {"dp": wide[c][0]}
            )
            arrive("sumfar", c, r, 1)
            part[2, c, r, 1] = (part[2, c, r, 1].astype(F32) + far_plus[c, r].astype(F32)).astype(
                BF16
            )
            send(("sum", c, r, 1), part.at[2, c, r, 1], from_plus.at[c, r, 1], {"dp": wide[c][1]})
    for c in range(2):
        arrive("half", c, 1)
        arrive("half", c, 0)

    def row_sum(c, r, piece):
        return (
            part[0, c, r, piece].astype(F32)
            + from_minus[c, r, piece].astype(F32)
            + from_plus[c, r, piece].astype(F32)
        )

    for c in range(2):
        arrive("sum", c, 3, 0)
        arrive("sum", c, 3, 1)
        for piece in range(2):
            mid[c, 3, piece] = row_sum(c, 3, piece).astype(BF16)
            target = (mid_far_minus, mid_far_plus)[piece]
            send(("midfar", c, piece), mid.at[c, 3, piece], target.at[c], {"dp": near[c][piece]})
    for c in range(2):
        arrive("sum", c, 1, 0)
        arrive("sum", c, 1, 1)
        mid[c, 1, 1] = row_sum(c, 1, 1).astype(BF16)
        send(("mid", c, 1), mid.at[c, 1, 1], mid_minus.at[c, 1], {"dp": near[c][0]})
        arrive("sum", c, 2, 0)
        arrive("sum", c, 2, 1)
        mid[c, 2, 0] = row_sum(c, 2, 0).astype(BF16)
        send(("mid", c, 0), mid.at[c, 2, 0], mid_plus.at[c, 0], {"dp": near[c][1]})
    for c in range(2):
        arrive("midfar", c, 0)
        mid[c, 1, 0] = (row_sum(c, 1, 0) + mid_far_minus[c].astype(F32)).astype(BF16)
        send(("midsum", c, 0), mid.at[c, 1, 0], mid_minus.at[c, 0], {"dp": near[c][0]})
        arrive("midfar", c, 1)
        mid[c, 2, 1] = (row_sum(c, 2, 1) + mid_far_plus[c].astype(F32)).astype(BF16)
        send(("midsum", c, 1), mid.at[c, 2, 1], mid_plus.at[c, 1], {"dp": near[c][1]})
    for c in range(2):
        arrive("sum", c, 0, 0)
        arrive("sum", c, 0, 1)
        arrive("mid", c, 0)
        arrive("mid", c, 1)
        arrive("midsum", c, 0)
        arrive("midsum", c, 1)
        for piece in range(2):
            total = (
                row_sum(c, 0, piece)
                + mid_minus[c, piece].astype(F32)
                + mid_plus[c, piece].astype(F32)
            ).astype(BF16)
            for target in range(expert_count):
                finished[c, target, pl.ds(piece * SUB, SUB)] = total[
                    :, target * lanes : (target + 1) * lanes
                ]
        for offset in peers:
            target = lax.rem(expert + offset, expert_count)
            send(
                ("back", c, offset),
                finished.at[c, target],
                returned.at[c, expert],
                {"expert": target},
            )
        returned[c, expert] = finished[c, expert]

    last_copies = []
    for c in range(2):
        for offset in peers:
            arrive("back", c, offset)
        for piece in range(2):
            window = pl.ds(piece * SUB, SUB)
            totals = [jnp.zeros((SUB, lanes), F32) for _ in range(4)]
            for source in range(expert_count):
                values = returned[c, source, window].astype(F32)
                block = pick[source, pair]
                scale = jnp.where(live[source, pair] == 1, weight[source, pair], 0.0)
                for slot in range(4):
                    totals[slot] = totals[slot] + jnp.where(block == slot, scale, 0.0) * values
            for slot in range(4):
                merged[slot, c, window] = totals[slot].astype(BF16)
        send(
            ("final", c),
            merged.at[pl.ds(2 * (1 - half), 2), c],
            out.at[:, half, c],
            {"dp": partner},
        )
        last_copies.append(
            pltpu.make_async_copy(
                merged.at[pl.ds(2 * half, 2), c], out.at[:, half, c], local_sem.at[2 + c]
            )
        )
        last_copies[c].start()
    for key, copy in copies.items():
        copy.wait_send()
    for c in range(2):
        last_copies[c].wait()
        arrive("final", c)


def on_device(tokens, w_gate, w_up, w_down, pick_block, pick_live, combine_weight):
    expert_count = lax.axis_size("expert")
    lanes = tokens.shape[1]
    width = lanes * expert_count
    group = w_gate.shape[2]
    hid_tiles = group // 128
    hbm = pl.BlockSpec(memory_space=pl.ANY)
    smem = pl.BlockSpec(memory_space=pltpu.SMEM)
    copy_count = 144
    result = pl.pallas_call(
        functools.partial(layer_kernel, expert_count),
        out_shape=jax.ShapeDtypeStruct((2, 2, 2, HALF // 2, lanes), BF16),
        in_specs=[hbm, hbm, hbm, hbm, smem, smem, smem],
        out_specs=hbm,
        scratch_shapes=[
            pltpu.VMEM((4, HALF // 2, lanes), BF16),
            pltpu.VMEM((4, HALF // 2, lanes), BF16),
            pltpu.VMEM((2, expert_count, HALF // 2, lanes), BF16),
            pltpu.VMEM((2, expert_count, HALF // 2, lanes), BF16),
            pltpu.VMEM((RING, 2, RING, 2, SUB, width), BF16),
            pltpu.VMEM((hid_tiles, width, 256), BF16),
            pltpu.VMEM((group, width), BF16),
            pltpu.VMEM((2 * RING * 2 * SUB, group), BF16),
            pltpu.VMEM((RING, 2, RING, 2, SUB, width), BF16),
            pltpu.VMEM((2, RING, 2, SUB, width), BF16),
            pltpu.VMEM((2, RING, 2, SUB, width), BF16),
            pltpu.VMEM((2, RING, SUB, width), BF16),
            pltpu.VMEM((2, RING, SUB, width), BF16),
            pltpu.VMEM((2, RING, 2, SUB, width), BF16),
            pltpu.VMEM((2, 2, SUB, width), BF16),
            pltpu.VMEM((2, 2, SUB, width), BF16),
            pltpu.VMEM((2, SUB, width), BF16),
            pltpu.VMEM((2, SUB, width), BF16),
            pltpu.VMEM((2, expert_count, HALF // 2, lanes), BF16),
            pltpu.VMEM((2, expert_count, HALF // 2, lanes), BF16),
            pltpu.VMEM((4, 2, HALF // 2, lanes), BF16),
            pltpu.SemaphoreType.DMA((copy_count,)),
            pltpu.SemaphoreType.DMA((copy_count,)),
            pltpu.SemaphoreType.DMA((2 * hid_tiles + 1,)),
            pltpu.SemaphoreType.DMA((4,)),
        ],
        compiler_params=pltpu.CompilerParams(
            collective_id=0, has_side_effects=True, vmem_limit_bytes=60 * 1024 * 1024
        ),
        name="moe_layer",
    )(
        tokens.reshape(2, 2, 2, HALF // 2, lanes),
        w_gate[0],
        w_up[0],
        w_down[0],
        pick_block,
        pick_live,
        combine_weight,
    )
    return result.reshape(tokens.shape)


def solution(mesh):
    in_specs = (
        P("dp", "expert"),
        P("expert", None, "dp"),
        P("expert", None, "dp"),
        P("expert", "dp", None),
        P(),
        P(),
        P(),
    )
    return jax.shard_map(
        on_device, mesh=mesh, in_specs=in_specs, out_specs=P("dp", "expert"), check_vma=False
    )
```

```python
import functools

import jax
import jax.numpy as jnp
from jax import lax
from jax.experimental import pallas as pl
from jax.experimental.pallas import tpu as pltpu
from jax.sharding import PartitionSpec as P

BLOCK = 128
HALF = BLOCK // 2
SUB = 16
RING = 4
DOWN = 512
BF16 = jnp.bfloat16
F32 = jnp.float32


def layer_kernel(
    expert_count,
    tok,
    w_gate,
    w_up,
    w_down,
    pick,
    live,
    weight,
    out,
    pair_first,
    pair_second,
    send_buf,
    arrived,
    rows,
    w_gu,
    w_dn,
    hidden,
    part,
    from_minus,
    from_plus,
    far_minus,
    far_plus,
    mid,
    mid_minus,
    mid_plus,
    mid_far_minus,
    mid_far_plus,
    finished,
    returned,
    merged,
    send_sem,
    recv_sem,
    weight_sem,
    local_sem,
):
    position = lax.axis_index("dp")
    expert = lax.axis_index("expert")
    x = lax.rem(position, RING)
    y = position // RING
    half = lax.rem(position, 2)
    pair = position // 2
    partner = position + 1 - 2 * half
    x_plus = y * RING + lax.rem(x + 1, RING)
    x_minus = y * RING + lax.rem(x + RING - 1, RING)
    y_plus = lax.rem(y + 1, RING) * RING + x
    y_minus = lax.rem(y + RING - 1, RING) * RING + x
    near = ((x_plus, x_minus), (y_plus, y_minus))
    wide = ((y_plus, y_minus), (x_plus, x_minus))
    lanes = tok.shape[-1]
    width = lanes * expert_count
    hid_tiles = w_gate.shape[1] // 128
    peers = (4, 3, 5, 2, 6, 1, 7)

    weight_copies = []
    for tile in range(hid_tiles):
        for which, source in enumerate((w_gate, w_up)):
            weight_copies.append(
                pltpu.make_async_copy(
                    source.at[:, pl.ds(tile * 128, 128)],
                    w_gu.at[tile, :, pl.ds(which * 128, 128)],
                    weight_sem.at[2 * tile + which],
                )
            )
    weight_copies.append(pltpu.make_async_copy(w_down, w_dn, weight_sem.at[2 * hid_tiles]))

    pair_bufs = (pair_first, pair_second)
    barrier = pltpu.get_barrier_semaphore()
    for target in (x_plus, x_minus, y_plus, y_minus):
        pl.semaphore_signal(
            barrier, inc=1, device_id={"dp": target}, device_id_type=pl.DeviceIdType.MESH
        )
    for offset in peers:
        pl.semaphore_signal(
            barrier,
            inc=1,
            device_id={"expert": lax.rem(expert + offset, expert_count)},
            device_id_type=pl.DeviceIdType.MESH,
        )
    pl.semaphore_wait(barrier, 4 + len(peers))

    copies = {}

    def send(key, source, target, device):
        number = len(copies)
        copy = pltpu.make_async_remote_copy(
            src_ref=source,
            dst_ref=target,
            send_sem=send_sem.at[number],
            recv_sem=recv_sem.at[number],
            device_id=device,
            device_id_type=pl.DeviceIdType.MESH,
        )
        copy.start()
        copies[key] = copy

    def arrive(*key):
        copies[key].wait_recv()

    for c in range(2):
        send(
            ("pair", c),
            tok.at[:, 1 - half, c],
            pair_bufs[c].at[pl.ds(2 * half, 2)],
            {"dp": partner},
        )
    own_copies = [
        pltpu.make_async_copy(
            tok.at[:, half, c], pair_bufs[c].at[pl.ds(2 * half, 2)], local_sem.at[c]
        )
        for c in range(2)
    ]
    for copy in own_copies:
        copy.start()

    def choose(target, c):
        chosen = pair_bufs[c][pick[target, pair]].astype(F32)
        return (chosen * live[target, pair].astype(F32)).astype(BF16)

    def spread_experts(c):
        own_copies[c].wait()
        arrive("pair", c)
        for offset in peers:
            target = lax.rem(expert + offset, expert_count)
            send_buf[c, offset] = choose(target, c)
            send(
                ("out", c, offset),
                send_buf.at[c, offset],
                arrived.at[c, expert],
                {"expert": target},
            )
        arrived[c, expert] = choose(expert, c)

    spread_experts(0)
    for copy in weight_copies:
        copy.start()

    def normalise(c):
        for piece in range(2):
            window = pl.ds(piece * SUB, SUB)
            square_sum = jnp.zeros((SUB, 1), F32)
            for source in range(expert_count):
                values = arrived[c, source, window].astype(F32)
                square_sum += jnp.sum(values * values, axis=1, keepdims=True)
            inv_rms = lax.rsqrt(square_sum / width + 1e-05)
            for source in range(expert_count):
                values = arrived[c, source, window].astype(F32)
                rows[0, c, 0, piece, :, pl.ds(source * lanes, lanes)] = (values * inv_rms).astype(
                    BF16
                )

    def spread_wide(c, r):
        send(("rows", 2, c, r), rows.at[0, c, r], rows.at[2, c, r], {"dp": wide[c][0]})
        send(("rows", 1, c, r), rows.at[0, c, r], rows.at[1, c, r], {"dp": wide[c][1]})

    def forward_wide(c, r):
        arrive("rows", 2, c, r)
        send(("far", c, r, 0), rows.at[2, c, r, 0], rows.at[3, c, r, 0], {"dp": wide[c][0]})
        arrive("rows", 1, c, r)
        send(("far", c, r, 1), rows.at[1, c, r, 1], rows.at[3, c, r, 1], {"dp": wide[c][1]})

    def experts(groups, slots):
        shape = (len(groups), 2, len(slots), 2, SUB)
        count = len(groups) * len(slots) * 4 * SUB
        groups = pl.ds(groups[0], len(groups))
        slots = pl.ds(slots[0], len(slots))
        batch = rows[groups, :, slots].reshape(count, width)
        for tile in range(hid_tiles):
            both = jnp.dot(batch, w_gu[tile], preferred_element_type=F32)
            gate = both[:, :128]
            value = gate * (1.0 / (1.0 + jnp.exp(-gate))) * both[:, 128:]
            hidden[:count, tile * 128 : (tile + 1) * 128] = value.astype(BF16)
        for tile in range(width // DOWN):
            columns = pl.ds(tile * DOWN, DOWN)
            value = jnp.dot(hidden[:count], w_dn[:, columns], preferred_element_type=F32)
            part[groups, :, slots, :, :, columns] = value.astype(BF16).reshape(*shape, DOWN)

    for c in range(2):
        for offset in peers:
            arrive("out", c, offset)
        normalise(c)
        send(("near", c, 2), rows.at[0, c, 0], rows.at[0, c, 2], {"dp": near[c][0]})
        send(("near", c, 1), rows.at[0, c, 0], rows.at[0, c, 1], {"dp": near[c][1]})
        spread_wide(c, 0)
        if c == 0:
            spread_experts(1)
    for c in range(2):
        arrive("near", c, 2)
        send(("nearfar", c, 0), rows.at[0, c, 2, 0], rows.at[0, c, 3, 0], {"dp": near[c][0]})
        arrive("near", c, 1)
        send(("nearfar", c, 1), rows.at[0, c, 1, 1], rows.at[0, c, 3, 1], {"dp": near[c][1]})
    for r in (1, 2):
        for c in range(2):
            spread_wide(c, r)
    for c in range(2):
        arrive("nearfar", c, 0)
        arrive("nearfar", c, 1)
        spread_wide(c, 3)
    for c in range(2):
        forward_wide(c, 0)
    for copy in weight_copies:
        copy.wait()
    experts((0,), (0, 1, 2, 3))
    for c in range(2):
        forward_wide(c, 1)
    experts((1, 2), (0, 1))
    for r in (2, 3):
        for c in range(2):
            forward_wide(c, r)
    experts((1, 2), (2, 3))
    for c in range(2):
        send(("half", c, 1), part.at[1, c, :, 1], from_minus.at[c, :, 1], {"dp": wide[c][0]})
        send(("half", c, 0), part.at[2, c, :, 0], from_plus.at[c, :, 0], {"dp": wide[c][1]})
    for slots in ((0, 1), (2, 3)):
        for r in slots:
            for c in range(2):
                arrive("far", c, r, 0)
                arrive("far", c, r, 1)
        experts((3,), slots)
        for r in reversed(slots):
            for c in range(2):
                send(
                    ("sumfar", c, r, 0),
                    part.at[3, c, r, 0],
                    far_minus.at[c, r],
                    {"dp": wide[c][0]},
                )
                send(
                    ("sumfar", c, r, 1), part.at[3, c, r, 1], far_plus.at[c, r], {"dp": wide[c][1]}
                )
    order = (1, 3, 2, 0)
    for r in order:
        for c in range(2):
            arrive("sumfar", c, r, 0)
            part[1, c, r, 0] = (part[1, c, r, 0].astype(F32) + far_minus[c, r].astype(F32)).astype(
                BF16
            )
            send(
                ("sum", c, r, 0), part.at[1, c, r, 0], from_minus.at[c, r, 0], {"dp": wide[c][0]}
            )
            arrive("sumfar", c, r, 1)
            part[2, c, r, 1] = (part[2, c, r, 1].astype(F32) + far_plus[c, r].astype(F32)).astype(
                BF16
            )
            send(("sum", c, r, 1), part.at[2, c, r, 1], from_plus.at[c, r, 1], {"dp": wide[c][1]})
    for c in range(2):
        arrive("half", c, 1)
        arrive("half", c, 0)

    def row_sum(c, r, piece):
        return (
            part[0, c, r, piece].astype(F32)
            + from_minus[c, r, piece].astype(F32)
            + from_plus[c, r, piece].astype(F32)
        )

    for c in range(2):
        arrive("sum", c, 3, 0)
        arrive("sum", c, 3, 1)
        for piece in range(2):
            mid[c, 3, piece] = row_sum(c, 3, piece).astype(BF16)
            target = (mid_far_minus, mid_far_plus)[piece]
            send(("midfar", c, piece), mid.at[c, 3, piece], target.at[c], {"dp": near[c][piece]})
    for c in range(2):
        arrive("sum", c, 1, 0)
        arrive("sum", c, 1, 1)
        mid[c, 1, 1] = row_sum(c, 1, 1).astype(BF16)
        send(("mid", c, 1), mid.at[c, 1, 1], mid_minus.at[c, 1], {"dp": near[c][0]})
        arrive("sum", c, 2, 0)
        arrive("sum", c, 2, 1)
        mid[c, 2, 0] = row_sum(c, 2, 0).astype(BF16)
        send(("mid", c, 0), mid.at[c, 2, 0], mid_plus.at[c, 0], {"dp": near[c][1]})
    for c in range(2):
        arrive("midfar", c, 0)
        mid[c, 1, 0] = (row_sum(c, 1, 0) + mid_far_minus[c].astype(F32)).astype(BF16)
        send(("midsum", c, 0), mid.at[c, 1, 0], mid_minus.at[c, 0], {"dp": near[c][0]})
        arrive("midfar", c, 1)
        mid[c, 2, 1] = (row_sum(c, 2, 1) + mid_far_plus[c].astype(F32)).astype(BF16)
        send(("midsum", c, 1), mid.at[c, 2, 1], mid_plus.at[c, 1], {"dp": near[c][1]})
    for c in range(2):
        arrive("sum", c, 0, 0)
        arrive("sum", c, 0, 1)
        arrive("mid", c, 0)
        arrive("mid", c, 1)
        arrive("midsum", c, 0)
        arrive("midsum", c, 1)
        for piece in range(2):
            total = (
                row_sum(c, 0, piece)
                + mid_minus[c, piece].astype(F32)
                + mid_plus[c, piece].astype(F32)
            ).astype(BF16)
            for target in range(expert_count):
                finished[c, target, pl.ds(piece * SUB, SUB)] = total[
                    :, target * lanes : (target + 1) * lanes
                ]
        for offset in peers:
            target = lax.rem(expert + offset, expert_count)
            send(
                ("back", c, offset),
                finished.at[c, target],
                returned.at[c, expert],
                {"expert": target},
            )
        returned[c, expert] = finished[c, expert]

    last_copies = []
    for c in range(2):
        for offset in peers:
            arrive("back", c, offset)
        for piece in range(2):
            window = pl.ds(piece * SUB, SUB)
            totals = [jnp.zeros((SUB, lanes), F32) for _ in range(4)]
            for source in range(expert_count):
                values = returned[c, source, window].astype(F32)
                block = pick[source, pair]
                scale = jnp.where(live[source, pair] == 1, weight[source, pair], 0.0)
                for slot in range(4):
                    totals[slot] = totals[slot] + jnp.where(block == slot, scale, 0.0) * values
            for slot in range(4):
                merged[slot, c, window] = totals[slot].astype(BF16)
        send(
            ("final", c),
            merged.at[pl.ds(2 * (1 - half), 2), c],
            out.at[:, half, c],
            {"dp": partner},
        )
        last_copies.append(
            pltpu.make_async_copy(
                merged.at[pl.ds(2 * half, 2), c], out.at[:, half, c], local_sem.at[2 + c]
            )
        )
        last_copies[c].start()
    for key, copy in copies.items():
        copy.wait_send()
    for c in range(2):
        last_copies[c].wait()
        arrive("final", c)


def on_device(tokens, w_gate, w_up, w_down, pick_block, pick_live, combine_weight):
    expert_count = lax.axis_size("expert")
    lanes = tokens.shape[1]
    width = lanes * expert_count
    group = w_gate.shape[2]
    hid_tiles = group // 128
    hbm = pl.BlockSpec(memory_space=pl.ANY)
    smem = pl.BlockSpec(memory_space=pltpu.SMEM)
    copy_count = 144
    result = pl.pallas_call(
        functools.partial(layer_kernel, expert_count),
        out_shape=jax.ShapeDtypeStruct((2, 2, 2, HALF // 2, lanes), BF16),
        in_specs=[hbm, hbm, hbm, hbm, smem, smem, smem],
        out_specs=hbm,
        scratch_shapes=[
            pltpu.VMEM((4, HALF // 2, lanes), BF16),
            pltpu.VMEM((4, HALF // 2, lanes), BF16),
            pltpu.VMEM((2, expert_count, HALF // 2, lanes), BF16),
            pltpu.VMEM((2, expert_count, HALF // 2, lanes), BF16),
            pltpu.VMEM((RING, 2, RING, 2, SUB, width), BF16),
            pltpu.VMEM((hid_tiles, width, 256), BF16),
            pltpu.VMEM((group, width), BF16),
            pltpu.VMEM((2 * RING * 2 * SUB, group), BF16),
            pltpu.VMEM((RING, 2, RING, 2, SUB, width), BF16),
            pltpu.VMEM((2, RING, 2, SUB, width), BF16),
            pltpu.VMEM((2, RING, 2, SUB, width), BF16),
            pltpu.VMEM((2, RING, SUB, width), BF16),
            pltpu.VMEM((2, RING, SUB, width), BF16),
            pltpu.VMEM((2, RING, 2, SUB, width), BF16),
            pltpu.VMEM((2, 2, SUB, width), BF16),
            pltpu.VMEM((2, 2, SUB, width), BF16),
            pltpu.VMEM((2, SUB, width), BF16),
            pltpu.VMEM((2, SUB, width), BF16),
            pltpu.VMEM((2, expert_count, HALF // 2, lanes), BF16),
            pltpu.VMEM((2, expert_count, HALF // 2, lanes), BF16),
            pltpu.VMEM((4, 2, HALF // 2, lanes), BF16),
            pltpu.SemaphoreType.DMA((copy_count,)),
            pltpu.SemaphoreType.DMA((copy_count,)),
            pltpu.SemaphoreType.DMA((2 * hid_tiles + 1,)),
            pltpu.SemaphoreType.DMA((4,)),
        ],
        compiler_params=pltpu.CompilerParams(
            collective_id=0, has_side_effects=True, vmem_limit_bytes=60 * 1024 * 1024
        ),
        name="moe_layer",
    )(
        tokens.reshape(2, 2, 2, HALF // 2, lanes),
        w_gate[0],
        w_up[0],
        w_down[0],
        pick_block,
        pick_live,
        combine_weight,
    )
    return result.reshape(tokens.shape)


def solution(mesh):
    in_specs = (
        P("dp", "expert"),
        P("expert", None, "dp"),
        P("expert", None, "dp"),
        P("expert", "dp", None),
        P(),
        P(),
        P(),
    )
    return jax.shard_map(
        on_device, mesh=mesh, in_specs=in_specs, out_specs=P("dp", "expert"), check_vma=False
    )
```

```python
import functools

import jax
import jax.numpy as jnp
from jax import lax
from jax.experimental import pallas as pl
from jax.experimental.pallas import tpu as pltpu
from jax.sharding import PartitionSpec as P

BLOCK = 128
HALF = BLOCK // 2
SUB = 16
RING = 4
DOWN = 512
BF16 = jnp.bfloat16
F32 = jnp.float32


def layer_kernel(
    expert_count,
    tok,
    w_gate,
    w_up,
    w_down,
    pick_hbm,
    live_hbm,
    weight_hbm,
    out,
    pick,
    live,
    weight,
    pair_first,
    pair_second,
    send_buf,
    arrived,
    rows,
    w_gu,
    w_dn,
    hidden,
    part,
    from_minus,
    from_plus,
    far_minus,
    far_plus,
    mid,
    mid_minus,
    mid_plus,
    mid_far_minus,
    mid_far_plus,
    finished,
    returned,
    merged,
    send_sem,
    recv_sem,
    weight_sem,
    local_sem,
):
    position = lax.axis_index("dp")
    expert = lax.axis_index("expert")
    x = lax.rem(position, RING)
    y = position // RING
    half = lax.rem(position, 2)
    pair = position // 2
    partner = position + 1 - 2 * half
    x_plus = y * RING + lax.rem(x + 1, RING)
    x_minus = y * RING + lax.rem(x + RING - 1, RING)
    y_plus = lax.rem(y + 1, RING) * RING + x
    y_minus = lax.rem(y + RING - 1, RING) * RING + x
    near = ((x_plus, x_minus), (y_plus, y_minus))
    wide = ((y_plus, y_minus), (x_plus, x_minus))
    lanes = tok.shape[-1]
    width = lanes * expert_count
    hid_tiles = w_gate.shape[1] // 128
    peers = (4, 3, 5, 2, 6, 1, 7)

    weight_copies = []
    for tile in range(hid_tiles):
        for which, source in enumerate((w_gate, w_up)):
            weight_copies.append(
                pltpu.make_async_copy(
                    source.at[:, pl.ds(tile * 128, 128)],
                    w_gu.at[tile, :, pl.ds(which * 128, 128)],
                    weight_sem.at[2 * tile + which],
                )
            )
    weight_copies.append(pltpu.make_async_copy(w_down, w_dn, weight_sem.at[2 * hid_tiles]))

    pair_bufs = (pair_first, pair_second)
    table_copies = [
        pltpu.make_async_copy(source, table, local_sem.at[4 + number])
        for number, (source, table) in enumerate(
            ((pick_hbm, pick), (live_hbm, live), (weight_hbm, weight))
        )
    ]
    own_copies = [
        pltpu.make_async_copy(
            tok.at[:, half, c], pair_bufs[c].at[pl.ds(2 * half, 2)], local_sem.at[c]
        )
        for c in range(2)
    ]
    for copy in table_copies + own_copies:
        copy.start()

    barrier = pltpu.get_barrier_semaphore()
    for target in (x_plus, x_minus, y_plus, y_minus):
        pl.semaphore_signal(
            barrier, inc=1, device_id={"dp": target}, device_id_type=pl.DeviceIdType.MESH
        )
    for offset in peers:
        pl.semaphore_signal(
            barrier,
            inc=1,
            device_id={"expert": lax.rem(expert + offset, expert_count)},
            device_id_type=pl.DeviceIdType.MESH,
        )
    pl.semaphore_wait(barrier, 4 + len(peers))

    copies = {}

    def send(key, source, target, device):
        number = len(copies)
        copy = pltpu.make_async_remote_copy(
            src_ref=source,
            dst_ref=target,
            send_sem=send_sem.at[number],
            recv_sem=recv_sem.at[number],
            device_id=device,
            device_id_type=pl.DeviceIdType.MESH,
        )
        copy.start()
        copies[key] = copy

    def arrive(*key):
        copies[key].wait_recv()

    for c in range(2):
        send(
            ("pair", c),
            tok.at[:, 1 - half, c],
            pair_bufs[c].at[pl.ds(2 * half, 2)],
            {"dp": partner},
        )
    for copy in table_copies:
        copy.wait()

    def choose(target, c):
        chosen = pair_bufs[c][pick[target, pair]].astype(F32)
        return (chosen * live[target, pair].astype(F32)).astype(BF16)

    def spread_experts(c):
        own_copies[c].wait()
        arrive("pair", c)
        for offset in peers:
            target = lax.rem(expert + offset, expert_count)
            send_buf[c, offset] = choose(target, c)
            send(
                ("out", c, offset),
                send_buf.at[c, offset],
                arrived.at[c, expert],
                {"expert": target},
            )
        arrived[c, expert] = choose(expert, c)

    spread_experts(0)
    for copy in weight_copies:
        copy.start()

    def normalise(c):
        for piece in range(2):
            window = pl.ds(piece * SUB, SUB)
            square_sum = jnp.zeros((SUB, 1), F32)
            for source in range(expert_count):
                values = arrived[c, source, window].astype(F32)
                square_sum += jnp.sum(values * values, axis=1, keepdims=True)
            inv_rms = lax.rsqrt(square_sum / width + 1e-05)
            for source in range(expert_count):
                values = arrived[c, source, window].astype(F32)
                rows[0, c, 0, piece, :, pl.ds(source * lanes, lanes)] = (values * inv_rms).astype(
                    BF16
                )

    def spread_wide(c, r):
        send(("rows", 2, c, r), rows.at[0, c, r], rows.at[2, c, r], {"dp": wide[c][0]})
        send(("rows", 1, c, r), rows.at[0, c, r], rows.at[1, c, r], {"dp": wide[c][1]})

    def forward_wide(c, r):
        arrive("rows", 2, c, r)
        send(("far", c, r, 0), rows.at[2, c, r, 0], rows.at[3, c, r, 0], {"dp": wide[c][0]})
        arrive("rows", 1, c, r)
        send(("far", c, r, 1), rows.at[1, c, r, 1], rows.at[3, c, r, 1], {"dp": wide[c][1]})

    def experts(groups, slots):
        shape = (len(groups), 2, len(slots), 2, SUB)
        count = len(groups) * len(slots) * 4 * SUB
        groups = pl.ds(groups[0], len(groups))
        slots = pl.ds(slots[0], len(slots))
        batch = rows[groups, :, slots].reshape(count, width)
        for tile in range(hid_tiles):
            both = jnp.dot(batch, w_gu[tile], preferred_element_type=F32)
            gate = both[:, :128]
            value = gate * (1.0 / (1.0 + jnp.exp(-gate))) * both[:, 128:]
            hidden[:count, tile * 128 : (tile + 1) * 128] = value.astype(BF16)
        for tile in range(width // DOWN):
            columns = pl.ds(tile * DOWN, DOWN)
            value = jnp.dot(hidden[:count], w_dn[:, columns], preferred_element_type=F32)
            part[groups, :, slots, :, :, columns] = value.astype(BF16).reshape(*shape, DOWN)

    for c in range(2):
        for offset in peers:
            arrive("out", c, offset)
        normalise(c)
        send(("near", c, 2), rows.at[0, c, 0], rows.at[0, c, 2], {"dp": near[c][0]})
        send(("near", c, 1), rows.at[0, c, 0], rows.at[0, c, 1], {"dp": near[c][1]})
        spread_wide(c, 0)
        if c == 0:
            spread_experts(1)
    for c in range(2):
        arrive("near", c, 2)
        send(("nearfar", c, 0), rows.at[0, c, 2, 0], rows.at[0, c, 3, 0], {"dp": near[c][0]})
        arrive("near", c, 1)
        send(("nearfar", c, 1), rows.at[0, c, 1, 1], rows.at[0, c, 3, 1], {"dp": near[c][1]})
    for r in (1, 2):
        for c in range(2):
            spread_wide(c, r)
    for c in range(2):
        arrive("nearfar", c, 0)
        arrive("nearfar", c, 1)
        spread_wide(c, 3)
    for c in range(2):
        forward_wide(c, 0)
    for copy in weight_copies:
        copy.wait()
    experts((0,), (0, 1, 2, 3))
    for c in range(2):
        forward_wide(c, 1)
    experts((1, 2), (0, 1))
    for r in (2, 3):
        for c in range(2):
            forward_wide(c, r)
    experts((1, 2), (2, 3))
    for c in range(2):
        send(("half", c, 1), part.at[1, c, :, 1], from_minus.at[c, :, 1], {"dp": wide[c][0]})
        send(("half", c, 0), part.at[2, c, :, 0], from_plus.at[c, :, 0], {"dp": wide[c][1]})
    for slots in ((0, 1), (2, 3)):
        for r in slots:
            for c in range(2):
                arrive("far", c, r, 0)
                arrive("far", c, r, 1)
        experts((3,), slots)
        for r in reversed(slots):
            for c in range(2):
                send(
                    ("sumfar", c, r, 0),
                    part.at[3, c, r, 0],
                    far_minus.at[c, r],
                    {"dp": wide[c][0]},
                )
                send(
                    ("sumfar", c, r, 1), part.at[3, c, r, 1], far_plus.at[c, r], {"dp": wide[c][1]}
                )
    order = (1, 3, 2, 0)
    for r in order:
        for c in range(2):
            arrive("sumfar", c, r, 0)
            part[1, c, r, 0] = (part[1, c, r, 0].astype(F32) + far_minus[c, r].astype(F32)).astype(
                BF16
            )
            send(
                ("sum", c, r, 0), part.at[1, c, r, 0], from_minus.at[c, r, 0], {"dp": wide[c][0]}
            )
            arrive("sumfar", c, r, 1)
            part[2, c, r, 1] = (part[2, c, r, 1].astype(F32) + far_plus[c, r].astype(F32)).astype(
                BF16
            )
            send(("sum", c, r, 1), part.at[2, c, r, 1], from_plus.at[c, r, 1], {"dp": wide[c][1]})
    for c in range(2):
        arrive("half", c, 1)
        arrive("half", c, 0)

    def row_sum(c, r, piece):
        return (
            part[0, c, r, piece].astype(F32)
            + from_minus[c, r, piece].astype(F32)
            + from_plus[c, r, piece].astype(F32)
        )

    for c in range(2):
        arrive("sum", c, 3, 0)
        arrive("sum", c, 3, 1)
        for piece in range(2):
            mid[c, 3, piece] = row_sum(c, 3, piece).astype(BF16)
            target = (mid_far_minus, mid_far_plus)[piece]
            send(("midfar", c, piece), mid.at[c, 3, piece], target.at[c], {"dp": near[c][piece]})
    for c in range(2):
        arrive("sum", c, 1, 0)
        arrive("sum", c, 1, 1)
        mid[c, 1, 1] = row_sum(c, 1, 1).astype(BF16)
        send(("mid", c, 1), mid.at[c, 1, 1], mid_minus.at[c, 1], {"dp": near[c][0]})
        arrive("sum", c, 2, 0)
        arrive("sum", c, 2, 1)
        mid[c, 2, 0] = row_sum(c, 2, 0).astype(BF16)
        send(("mid", c, 0), mid.at[c, 2, 0], mid_plus.at[c, 0], {"dp": near[c][1]})
    for c in range(2):
        arrive("midfar", c, 0)
        mid[c, 1, 0] = (row_sum(c, 1, 0) + mid_far_minus[c].astype(F32)).astype(BF16)
        send(("midsum", c, 0), mid.at[c, 1, 0], mid_minus.at[c, 0], {"dp": near[c][0]})
        arrive("midfar", c, 1)
        mid[c, 2, 1] = (row_sum(c, 2, 1) + mid_far_plus[c].astype(F32)).astype(BF16)
        send(("midsum", c, 1), mid.at[c, 2, 1], mid_plus.at[c, 1], {"dp": near[c][1]})
    for c in range(2):
        arrive("sum", c, 0, 0)
        arrive("sum", c, 0, 1)
        arrive("mid", c, 0)
        arrive("mid", c, 1)
        arrive("midsum", c, 0)
        arrive("midsum", c, 1)
        for piece in range(2):
            total = (
                row_sum(c, 0, piece)
                + mid_minus[c, piece].astype(F32)
                + mid_plus[c, piece].astype(F32)
            ).astype(BF16)
            for target in range(expert_count):
                finished[c, target, pl.ds(piece * SUB, SUB)] = total[
                    :, target * lanes : (target + 1) * lanes
                ]
        for offset in peers:
            target = lax.rem(expert + offset, expert_count)
            send(
                ("back", c, offset),
                finished.at[c, target],
                returned.at[c, expert],
                {"expert": target},
            )
        returned[c, expert] = finished[c, expert]

    last_copies = []
    for c in range(2):
        for offset in peers:
            arrive("back", c, offset)
        for piece in range(2):
            window = pl.ds(piece * SUB, SUB)
            totals = [jnp.zeros((SUB, lanes), F32) for _ in range(4)]
            for source in range(expert_count):
                values = returned[c, source, window].astype(F32)
                block = pick[source, pair]
                scale = jnp.where(live[source, pair] == 1, weight[source, pair], 0.0)
                for slot in range(4):
                    totals[slot] = totals[slot] + jnp.where(block == slot, scale, 0.0) * values
            for slot in range(4):
                merged[slot, c, window] = totals[slot].astype(BF16)
        send(
            ("final", c),
            merged.at[pl.ds(2 * (1 - half), 2), c],
            out.at[:, half, c],
            {"dp": partner},
        )
        last_copies.append(
            pltpu.make_async_copy(
                merged.at[pl.ds(2 * half, 2), c], out.at[:, half, c], local_sem.at[2 + c]
            )
        )
        last_copies[c].start()
    for key, copy in copies.items():
        copy.wait_send()
    for c in range(2):
        last_copies[c].wait()
        arrive("final", c)


def on_device(tokens, w_gate, w_up, w_down, pick_block, pick_live, combine_weight):
    expert_count = lax.axis_size("expert")
    lanes = tokens.shape[1]
    width = lanes * expert_count
    group = w_gate.shape[2]
    hid_tiles = group // 128
    hbm = pl.BlockSpec(memory_space=pltpu.HBM)
    copy_count = 144
    result = pl.pallas_call(
        functools.partial(layer_kernel, expert_count),
        out_shape=jax.ShapeDtypeStruct((2, 2, 2, HALF // 2, lanes), BF16),
        in_specs=[hbm] * 7,
        out_specs=pl.BlockSpec(memory_space=pl.ANY),
        scratch_shapes=[
            pltpu.SMEM(pick_block.shape, pick_block.dtype),
            pltpu.SMEM(pick_live.shape, pick_live.dtype),
            pltpu.SMEM(combine_weight.shape, combine_weight.dtype),
            pltpu.VMEM((4, HALF // 2, lanes), BF16),
            pltpu.VMEM((4, HALF // 2, lanes), BF16),
            pltpu.VMEM((2, expert_count, HALF // 2, lanes), BF16),
            pltpu.VMEM((2, expert_count, HALF // 2, lanes), BF16),
            pltpu.VMEM((RING, 2, RING, 2, SUB, width), BF16),
            pltpu.VMEM((hid_tiles, width, 256), BF16),
            pltpu.VMEM((group, width), BF16),
            pltpu.VMEM((2 * RING * 2 * SUB, group), BF16),
            pltpu.VMEM((RING, 2, RING, 2, SUB, width), BF16),
            pltpu.VMEM((2, RING, 2, SUB, width), BF16),
            pltpu.VMEM((2, RING, 2, SUB, width), BF16),
            pltpu.VMEM((2, RING, SUB, width), BF16),
            pltpu.VMEM((2, RING, SUB, width), BF16),
            pltpu.VMEM((2, RING, 2, SUB, width), BF16),
            pltpu.VMEM((2, 2, SUB, width), BF16),
            pltpu.VMEM((2, 2, SUB, width), BF16),
            pltpu.VMEM((2, SUB, width), BF16),
            pltpu.VMEM((2, SUB, width), BF16),
            pltpu.VMEM((2, expert_count, HALF // 2, lanes), BF16),
            pltpu.VMEM((2, expert_count, HALF // 2, lanes), BF16),
            pltpu.VMEM((4, 2, HALF // 2, lanes), BF16),
            pltpu.SemaphoreType.DMA((copy_count,)),
            pltpu.SemaphoreType.DMA((copy_count,)),
            pltpu.SemaphoreType.DMA((2 * hid_tiles + 1,)),
            pltpu.SemaphoreType.DMA((7,)),
        ],
        compiler_params=pltpu.CompilerParams(
            collective_id=0, has_side_effects=True, vmem_limit_bytes=60 * 1024 * 1024
        ),
        name="moe_layer",
    )(
        tokens.reshape(2, 2, 2, HALF // 2, lanes),
        w_gate[0],
        w_up[0],
        w_down[0],
        pick_block,
        pick_live,
        combine_weight,
    )
    return result.reshape(tokens.shape)


def solution(mesh):
    in_specs = (
        P("dp", "expert"),
        P("expert", None, "dp"),
        P("expert", None, "dp"),
        P("expert", "dp", None),
        P(),
        P(),
        P(),
    )
    return jax.shard_map(
        on_device, mesh=mesh, in_specs=in_specs, out_specs=P("dp", "expert"), check_vma=False
    )
```

```python
import functools

import jax
import jax.numpy as jnp
from jax import lax
from jax.experimental import pallas as pl
from jax.experimental.pallas import tpu as pltpu
from jax.sharding import PartitionSpec as P

BLOCK = 128
HALF = BLOCK // 2
SUB = 16
RING = 4
DOWN = 512
BF16 = jnp.bfloat16
F32 = jnp.float32


def layer_kernel(
    expert_count,
    tok,
    w_gate,
    w_up,
    w_down,
    pick_hbm,
    live_hbm,
    weight_hbm,
    out,
    pick,
    live,
    weight,
    pair_first,
    pair_second,
    send_buf,
    arrived,
    rows,
    w_gu,
    w_dn,
    hidden,
    part,
    from_minus,
    from_plus,
    far_minus,
    far_plus,
    mid,
    mid_minus,
    mid_plus,
    mid_far_minus,
    mid_far_plus,
    finished,
    returned,
    merged,
    send_sem,
    recv_sem,
    weight_sem,
    local_sem,
):
    position = lax.axis_index("dp")
    expert = lax.axis_index("expert")
    x = lax.rem(position, RING)
    y = position // RING
    half = lax.rem(position, 2)
    pair = position // 2
    partner = position + 1 - 2 * half
    x_plus = y * RING + lax.rem(x + 1, RING)
    x_minus = y * RING + lax.rem(x + RING - 1, RING)
    y_plus = lax.rem(y + 1, RING) * RING + x
    y_minus = lax.rem(y + RING - 1, RING) * RING + x
    near = ((x_plus, x_minus), (y_plus, y_minus))
    wide = ((y_plus, y_minus), (x_plus, x_minus))
    lanes = tok.shape[-1]
    width = lanes * expert_count
    hid_tiles = w_gate.shape[1] // 128
    peers = (4, 3, 5, 2, 6, 1, 7)

    weight_copies = []
    for tile in range(hid_tiles):
        for which, source in enumerate((w_gate, w_up)):
            weight_copies.append(
                pltpu.make_async_copy(
                    source.at[:, pl.ds(tile * 128, 128)],
                    w_gu.at[tile, :, pl.ds(which * 128, 128)],
                    weight_sem.at[2 * tile + which],
                )
            )
    weight_copies.append(pltpu.make_async_copy(w_down, w_dn, weight_sem.at[2 * hid_tiles]))

    pair_bufs = (pair_first, pair_second)
    table_copies = [
        pltpu.make_async_copy(source, table, local_sem.at[4 + number])
        for number, (source, table) in enumerate(
            ((pick_hbm, pick), (live_hbm, live), (weight_hbm, weight))
        )
    ]
    own_copies = [
        pltpu.make_async_copy(
            tok.at[:, half, c], pair_bufs[c].at[pl.ds(2 * half, 2)], local_sem.at[c]
        )
        for c in range(2)
    ]
    for copy in table_copies + own_copies:
        copy.start()

    barrier = pltpu.get_barrier_semaphore()
    for target in (x_plus, x_minus, y_plus, y_minus):
        pl.semaphore_signal(
            barrier, inc=1, device_id={"dp": target}, device_id_type=pl.DeviceIdType.MESH
        )
    for offset in peers:
        pl.semaphore_signal(
            barrier,
            inc=1,
            device_id={"expert": lax.rem(expert + offset, expert_count)},
            device_id_type=pl.DeviceIdType.MESH,
        )
    pl.semaphore_wait(barrier, 4 + len(peers))

    copies = {}

    def send(key, source, target, device):
        number = len(copies)
        copy = pltpu.make_async_remote_copy(
            src_ref=source,
            dst_ref=target,
            send_sem=send_sem.at[number],
            recv_sem=recv_sem.at[number],
            device_id=device,
            device_id_type=pl.DeviceIdType.MESH,
        )
        copy.start()
        copies[key] = copy

    def arrive(*key):
        copies[key].wait_recv()

    def swap(c):
        send(
            ("pair", c),
            tok.at[:, 1 - half, c],
            pair_bufs[c].at[pl.ds(2 * half, 2)],
            {"dp": partner},
        )

    swap(0)
    for copy in table_copies:
        copy.wait()

    def choose(target, c):
        chosen = pair_bufs[c][pick[target, pair]].astype(F32)
        return (chosen * live[target, pair].astype(F32)).astype(BF16)

    def spread_experts(c):
        own_copies[c].wait()
        arrive("pair", c)
        if c == 0:
            swap(1)
        for offset in peers:
            target = lax.rem(expert + offset, expert_count)
            send_buf[c, offset] = choose(target, c)
            send(
                ("out", c, offset),
                send_buf.at[c, offset],
                arrived.at[c, expert],
                {"expert": target},
            )
        arrived[c, expert] = choose(expert, c)

    spread_experts(0)
    for copy in weight_copies:
        copy.start()

    def normalise(c):
        for piece in range(2):
            window = pl.ds(piece * SUB, SUB)
            square_sum = jnp.zeros((SUB, 1), F32)
            for source in range(expert_count):
                values = arrived[c, source, window].astype(F32)
                square_sum += jnp.sum(values * values, axis=1, keepdims=True)
            inv_rms = lax.rsqrt(square_sum / width + 1e-05)
            for source in range(expert_count):
                values = arrived[c, source, window].astype(F32)
                rows[0, c, 0, piece, :, pl.ds(source * lanes, lanes)] = (values * inv_rms).astype(
                    BF16
                )

    def spread_wide(c, r):
        send(("rows", 2, c, r), rows.at[0, c, r], rows.at[2, c, r], {"dp": wide[c][0]})
        send(("rows", 1, c, r), rows.at[0, c, r], rows.at[1, c, r], {"dp": wide[c][1]})

    def forward_wide(c, r):
        arrive("rows", 2, c, r)
        send(("far", c, r, 0), rows.at[2, c, r, 0], rows.at[3, c, r, 0], {"dp": wide[c][0]})
        arrive("rows", 1, c, r)
        send(("far", c, r, 1), rows.at[1, c, r, 1], rows.at[3, c, r, 1], {"dp": wide[c][1]})

    def experts(groups, slots):
        shape = (len(groups), 2, len(slots), 2, SUB)
        count = len(groups) * len(slots) * 4 * SUB
        groups = pl.ds(groups[0], len(groups))
        slots = pl.ds(slots[0], len(slots))
        batch = rows[groups, :, slots].reshape(count, width)
        for tile in range(hid_tiles):
            both = jnp.dot(batch, w_gu[tile], preferred_element_type=F32)
            gate = both[:, :128]
            value = gate * (1.0 / (1.0 + jnp.exp(-gate))) * both[:, 128:]
            hidden[:count, tile * 128 : (tile + 1) * 128] = value.astype(BF16)
        for tile in range(width // DOWN):
            columns = pl.ds(tile * DOWN, DOWN)
            value = jnp.dot(hidden[:count], w_dn[:, columns], preferred_element_type=F32)
            part[groups, :, slots, :, :, columns] = value.astype(BF16).reshape(*shape, DOWN)

    for c in range(2):
        for offset in peers:
            arrive("out", c, offset)
        normalise(c)
        send(("near", c, 2), rows.at[0, c, 0], rows.at[0, c, 2], {"dp": near[c][0]})
        send(("near", c, 1), rows.at[0, c, 0], rows.at[0, c, 1], {"dp": near[c][1]})
        spread_wide(c, 0)
        if c == 0:
            spread_experts(1)
    for c in range(2):
        arrive("near", c, 2)
        send(("nearfar", c, 0), rows.at[0, c, 2, 0], rows.at[0, c, 3, 0], {"dp": near[c][0]})
        arrive("near", c, 1)
        send(("nearfar", c, 1), rows.at[0, c, 1, 1], rows.at[0, c, 3, 1], {"dp": near[c][1]})
    for c in range(2):
        spread_wide(c, 1)
    for c in range(2):
        arrive("nearfar", c, 0)
        arrive("nearfar", c, 1)
        spread_wide(c, 3)
    for c in range(2):
        spread_wide(c, 2)
    for c in range(2):
        forward_wide(c, 0)
    for copy in weight_copies:
        copy.wait()
    experts((0,), (0, 1, 2, 3))
    for c in range(2):
        forward_wide(c, 1)
    experts((1, 2), (0, 1))
    for r in (2, 3):
        for c in range(2):
            forward_wide(c, r)
    experts((1, 2), (2, 3))
    for c in range(2):
        send(("half", c, 1), part.at[1, c, :, 1], from_minus.at[c, :, 1], {"dp": wide[c][0]})
        send(("half", c, 0), part.at[2, c, :, 0], from_plus.at[c, :, 0], {"dp": wide[c][1]})
    for slots in ((0, 1), (2, 3)):
        for r in slots:
            for c in range(2):
                arrive("far", c, r, 0)
                arrive("far", c, r, 1)
        experts((3,), slots)
        for r in reversed(slots):
            for c in range(2):
                send(
                    ("sumfar", c, r, 0),
                    part.at[3, c, r, 0],
                    far_minus.at[c, r],
                    {"dp": wide[c][0]},
                )
                send(
                    ("sumfar", c, r, 1), part.at[3, c, r, 1], far_plus.at[c, r], {"dp": wide[c][1]}
                )
    order = (1, 3, 2, 0)
    for r in order:
        for c in range(2):
            arrive("sumfar", c, r, 0)
            part[1, c, r, 0] = (part[1, c, r, 0].astype(F32) + far_minus[c, r].astype(F32)).astype(
                BF16
            )
            send(
                ("sum", c, r, 0), part.at[1, c, r, 0], from_minus.at[c, r, 0], {"dp": wide[c][0]}
            )
            arrive("sumfar", c, r, 1)
            part[2, c, r, 1] = (part[2, c, r, 1].astype(F32) + far_plus[c, r].astype(F32)).astype(
                BF16
            )
            send(("sum", c, r, 1), part.at[2, c, r, 1], from_plus.at[c, r, 1], {"dp": wide[c][1]})
    for c in range(2):
        arrive("half", c, 1)
        arrive("half", c, 0)

    def row_sum(c, r, piece):
        return (
            part[0, c, r, piece].astype(F32)
            + from_minus[c, r, piece].astype(F32)
            + from_plus[c, r, piece].astype(F32)
        )

    for c in range(2):
        arrive("sum", c, 3, 0)
        arrive("sum", c, 3, 1)
        for piece in range(2):
            mid[c, 3, piece] = row_sum(c, 3, piece).astype(BF16)
            target = (mid_far_minus, mid_far_plus)[piece]
            send(("midfar", c, piece), mid.at[c, 3, piece], target.at[c], {"dp": near[c][piece]})
    for c in range(2):
        arrive("sum", c, 1, 0)
        arrive("sum", c, 1, 1)
        mid[c, 1, 1] = row_sum(c, 1, 1).astype(BF16)
        send(("mid", c, 1), mid.at[c, 1, 1], mid_minus.at[c, 1], {"dp": near[c][0]})
        arrive("sum", c, 2, 0)
        arrive("sum", c, 2, 1)
        mid[c, 2, 0] = row_sum(c, 2, 0).astype(BF16)
        send(("mid", c, 0), mid.at[c, 2, 0], mid_plus.at[c, 0], {"dp": near[c][1]})
    for c in range(2):
        arrive("midfar", c, 0)
        mid[c, 1, 0] = (row_sum(c, 1, 0) + mid_far_minus[c].astype(F32)).astype(BF16)
        send(("midsum", c, 0), mid.at[c, 1, 0], mid_minus.at[c, 0], {"dp": near[c][0]})
        arrive("midfar", c, 1)
        mid[c, 2, 1] = (row_sum(c, 2, 1) + mid_far_plus[c].astype(F32)).astype(BF16)
        send(("midsum", c, 1), mid.at[c, 2, 1], mid_plus.at[c, 1], {"dp": near[c][1]})
    for c in range(2):
        arrive("sum", c, 0, 0)
        arrive("sum", c, 0, 1)
        arrive("mid", c, 0)
        arrive("mid", c, 1)
        arrive("midsum", c, 0)
        arrive("midsum", c, 1)
        for piece in range(2):
            total = (
                row_sum(c, 0, piece)
                + mid_minus[c, piece].astype(F32)
                + mid_plus[c, piece].astype(F32)
            ).astype(BF16)
            for target in range(expert_count):
                finished[c, target, pl.ds(piece * SUB, SUB)] = total[
                    :, target * lanes : (target + 1) * lanes
                ]
        for offset in peers:
            target = lax.rem(expert + offset, expert_count)
            send(
                ("back", c, offset),
                finished.at[c, target],
                returned.at[c, expert],
                {"expert": target},
            )
        returned[c, expert] = finished[c, expert]

    last_copies = []
    for c in range(2):
        for offset in peers:
            arrive("back", c, offset)
        for piece in range(2):
            window = pl.ds(piece * SUB, SUB)
            totals = [jnp.zeros((SUB, lanes), F32) for _ in range(4)]
            for source in range(expert_count):
                values = returned[c, source, window].astype(F32)
                block = pick[source, pair]
                scale = jnp.where(live[source, pair] == 1, weight[source, pair], 0.0)
                for slot in range(4):
                    totals[slot] = totals[slot] + jnp.where(block == slot, scale, 0.0) * values
            for slot in range(4):
                merged[slot, c, window] = totals[slot].astype(BF16)
        send(
            ("final", c),
            merged.at[pl.ds(2 * (1 - half), 2), c],
            out.at[:, half, c],
            {"dp": partner},
        )
        last_copies.append(
            pltpu.make_async_copy(
                merged.at[pl.ds(2 * half, 2), c], out.at[:, half, c], local_sem.at[2 + c]
            )
        )
        last_copies[c].start()
    for key, copy in copies.items():
        copy.wait_send()
    for c in range(2):
        last_copies[c].wait()
        arrive("final", c)


def on_device(tokens, w_gate, w_up, w_down, pick_block, pick_live, combine_weight):
    expert_count = lax.axis_size("expert")
    lanes = tokens.shape[1]
    width = lanes * expert_count
    group = w_gate.shape[2]
    hid_tiles = group // 128
    hbm = pl.BlockSpec(memory_space=pltpu.HBM)
    copy_count = 144
    result = pl.pallas_call(
        functools.partial(layer_kernel, expert_count),
        out_shape=jax.ShapeDtypeStruct((2, 2, 2, HALF // 2, lanes), BF16),
        in_specs=[hbm] * 7,
        out_specs=pl.BlockSpec(memory_space=pl.ANY),
        scratch_shapes=[
            pltpu.SMEM(pick_block.shape, pick_block.dtype),
            pltpu.SMEM(pick_live.shape, pick_live.dtype),
            pltpu.SMEM(combine_weight.shape, combine_weight.dtype),
            pltpu.VMEM((4, HALF // 2, lanes), BF16),
            pltpu.VMEM((4, HALF // 2, lanes), BF16),
            pltpu.VMEM((2, expert_count, HALF // 2, lanes), BF16),
            pltpu.VMEM((2, expert_count, HALF // 2, lanes), BF16),
            pltpu.VMEM((RING, 2, RING, 2, SUB, width), BF16),
            pltpu.VMEM((hid_tiles, width, 256), BF16),
            pltpu.VMEM((group, width), BF16),
            pltpu.VMEM((2 * RING * 2 * SUB, group), BF16),
            pltpu.VMEM((RING, 2, RING, 2, SUB, width), BF16),
            pltpu.VMEM((2, RING, 2, SUB, width), BF16),
            pltpu.VMEM((2, RING, 2, SUB, width), BF16),
            pltpu.VMEM((2, RING, SUB, width), BF16),
            pltpu.VMEM((2, RING, SUB, width), BF16),
            pltpu.VMEM((2, RING, 2, SUB, width), BF16),
            pltpu.VMEM((2, 2, SUB, width), BF16),
            pltpu.VMEM((2, 2, SUB, width), BF16),
            pltpu.VMEM((2, SUB, width), BF16),
            pltpu.VMEM((2, SUB, width), BF16),
            pltpu.VMEM((2, expert_count, HALF // 2, lanes), BF16),
            pltpu.VMEM((2, expert_count, HALF // 2, lanes), BF16),
            pltpu.VMEM((4, 2, HALF // 2, lanes), BF16),
            pltpu.SemaphoreType.DMA((copy_count,)),
            pltpu.SemaphoreType.DMA((copy_count,)),
            pltpu.SemaphoreType.DMA((2 * hid_tiles + 1,)),
            pltpu.SemaphoreType.DMA((7,)),
        ],
        compiler_params=pltpu.CompilerParams(
            collective_id=0, has_side_effects=True, vmem_limit_bytes=60 * 1024 * 1024
        ),
        name="moe_layer",
    )(
        tokens.reshape(2, 2, 2, HALF // 2, lanes),
        w_gate[0],
        w_up[0],
        w_down[0],
        pick_block,
        pick_live,
        combine_weight,
    )
    return result.reshape(tokens.shape)


def solution(mesh):
    in_specs = (
        P("dp", "expert"),
        P("expert", None, "dp"),
        P("expert", None, "dp"),
        P("expert", "dp", None),
        P(),
        P(),
        P(),
    )
    return jax.shard_map(
        on_device, mesh=mesh, in_specs=in_specs, out_specs=P("dp", "expert"), check_vma=False
    )
```
